256 devices in a mesh: dp: 4 (over x), expert: 8 (over z), tensor: 8 (over y, core).
Axes of the slice: x: 4, y: 4, z: 8, core: 2. Of those that a mesh axis runs over, the one named last changes fastest.
Arguments:
- tokens: bfloat16 [1024, 6144], P('expert'), may hold values from -6 to 6
- routes: int32 [1024, 2], P('expert'), may hold values from 0 to 7, all different within a row; in each aligned block of 128 rows (0 to 127, 128 to 255, ...) at most 64 rows name the same one
- logits: float32 [1024, 2], P('expert'), may hold values from -8 to 8
- grad_out: bfloat16 [1024, 6144], P('expert'), may hold values from -6 to 6
- w_gate: bfloat16 [8, 6144, 8192], P('expert', None, ('dp', 'tensor')), may hold values from -0.078125 to 0.078125
- w_up: bfloat16 [8, 6144, 8192], P('expert', None, ('dp', 'tensor')), may hold values from -0.078125 to 0.078125
- w_down: bfloat16 [8, 8192, 6144], P('expert', ('dp', 'tensor')), may hold values from -0.0625 to 0.0625
Outputs:
- output: bfloat16 [1024, 6144], P(('expert', 'tensor'))
- grad_tokens: bfloat16 [1024, 6144], P(('expert', 'tensor'))
The draws below stay inside these ranges and needn't reach their ends.
Inputs may be any that keep to these rules, and one draw needn't show every extreme that they name: `routes`: each token names two different experts. The 128 tokens of one index of the expert axis name one expert at most 64 times, and in every draw some expert is named exactly 64 times by the tokens of some index.
All inputs are finite; a program needn't handle non-finite values.
Results may differ from the reference program's by a relative error of at most 0.015.
Values may be sent and summed in bfloat16 or wider, within the bound.
No kernel may reach another device: no remote copies, remote signals or barrier semaphores. Data moves between devices by JAX's collectives and lax.ppermute only.
A program may use at most 128 MiB of HBM per device.

```python
import math
import jax
import jax.numpy as jnp
import numpy as np
from jax import lax

D = 6144
FFW = 8192
TOK_DEV = 128
EXPERTS = 8
CAP = 64
TOKENS = 1024
N_DP = 4
N_TENSOR = 8


def steps_of(own_key, dims, pieces, least, top_value):
    gain = 1.0
    for position, blocks in pieces:
        heights = jax.random.uniform(jax.random.fold_in(jax.random.fold_in(own_key, 6), position), (blocks,), jnp.float32, least / len(pieces), top_value / len(pieces))
        gain = gain * jnp.repeat(jnp.exp(heights), dims[position] // blocks).reshape((-1,) + (1,) * (len(dims) - 1 - position))
    return gain


def assign_block(own_key, own, number, rows, number_of, top, limit, lean):
    ranking = jax.random.permutation(own_key, number_of)
    packed, ordinary = load_shares(number_of, rows * top, limit, lean, True), load_shares(number_of, rows * top, limit, lean, False)
    places = jnp.arange(number_of)

    def named(tallies, rotation):
        used = int((tallies > 0).sum())
        fixed = max(1, used // 4)
        passed = fixed + (places - fixed + rotation * (used - fixed)) % max(1, number_of - fixed)
        return jnp.zeros((number_of,), jnp.int32).at[ranking[jnp.where(places < fixed, places, passed)]].set(jnp.asarray(tallies, jnp.int32))

    tallies = jnp.where(number % 4 == 0, named(packed, number // 4), named(ordinary, number - number // 4 - 1))
    mixed = jax.random.permutation(jax.random.fold_in(own, 3), number_of)
    giver, sink = mixed[0:number_of // 2 * 2:2], mixed[1:number_of // 2 * 2:2]
    margin = jnp.minimum(tallies[giver] - 1, limit - tallies[sink]) // 2
    margin = jnp.where((giver == ranking[0]) | (sink == ranking[0]) | (tallies[sink] == 0), 0, jnp.maximum(margin, 0))
    passed = jax.random.randint(jax.random.fold_in(own, 4), (number_of // 2,), 0, 1 << 20) % (margin + 1)
    tallies = tallies.at[giver].add(-passed).at[sink].add(passed)
    members = jnp.searchsorted(jnp.cumsum(tallies), jnp.arange(rows * top), side="right").astype(jnp.int32)
    grid = members.reshape(top, rows).T
    grid = grid[jax.random.permutation(jax.random.fold_in(own, 1), rows)]
    rotation = jax.random.randint(jax.random.fold_in(own, 2), (rows, 1), 0, top)
    return jnp.take_along_axis(grid, (jnp.arange(top)[None, :] + rotation) % top, axis=1)


def load_shares(number_of, total, bound, skew, full):
    weights = [(1 << 20) // math.isqrt(grade ** skew) + 1 for grade in range(1, number_of + 1)]
    largest = bound if full else min(bound, max(-(-total // number_of), total * weights[0] // sum(weights)))
    least = 1 if total - largest >= number_of - 1 else 0
    given, spare = [largest] + [least] * (number_of - 1), total - largest - least * (number_of - 1)
    while spare > 0:
        candidates = [i for i in range(1, number_of) if given[i] < largest] or [i for i in range(1, number_of) if given[i] < bound]
        whole, budget = sum([weights[i] for i in candidates]), spare
        for i in candidates:
            more = min(bound - given[i], max(1, budget * weights[i] // whole), spare)
            given[i] = given[i] + more
            spare = spare - more
    return np.array(given)


def centred(own_key, shape, scale, most, shards=(), kind=jnp.bfloat16):
    result = jax.random.normal(own_key, shape, jnp.float32) * scale
    if len(shards) > 0:
        result = steps_of(own_key, shape, shards, -0.22, 0.18) * result
    return jnp.clip(result, min=-most, max=most).astype(kind)


def setup_inputs(seed: int = 0) -> dict:
    key_list = jax.random.split(jax.random.key(seed), 8)
    tokens = centred(key_list[0], (TOKENS, D), 1.0, 6.0, ((0, 8),))
    routes_keys = jax.random.split(jax.random.fold_in(key_list[1], 1), TOKENS // TOK_DEV)
    routes_turns = jax.random.permutation(jax.random.fold_in(key_list[1], 3), TOKENS // TOK_DEV)
    routes = jax.vmap(lambda own, number: assign_block(jax.random.fold_in(key_list[1], 2), own, number, TOK_DEV, EXPERTS, 2, CAP, 2))(routes_keys, routes_turns).reshape((TOKENS, 2))
    logits = centred(key_list[2], (TOKENS, 2), 2.0, 8.0, ((0, 8),), jnp.float32)
    grad_out = centred(key_list[3], (TOKENS, D), 1.0, 6.0, ((0, 8),))
    w_gate = centred(key_list[4], (EXPERTS, D, FFW), D ** -0.5, 0.078125, ((0, 8), (2, 32)))
    w_up = centred(key_list[5], (EXPERTS, D, FFW), D ** -0.5, 0.078125, ((0, 8), (2, 32)))
    w_down = centred(key_list[6], (EXPERTS, FFW, D), FFW ** -0.5, 0.0625, ((0, 8), (1, 32)))
    return dict(tokens=tokens, routes=routes, logits=logits, grad_out=grad_out, w_gate=w_gate, w_up=w_up, w_down=w_down)


def activate(gate, up):
    sig = jax.nn.sigmoid(gate)
    return (gate * sig * up).astype(jnp.bfloat16)


def backprop(grad_hidden, gate, up):
    sig = jax.nn.sigmoid(gate)
    grad_gate = (grad_hidden * up * sig * (1.0 + gate * (1.0 - sig))).astype(jnp.bfloat16)
    grad_up = (grad_hidden * gate * sig).astype(jnp.bfloat16)
    return grad_gate, grad_up


def round_term(term):
    narrow = lax.optimization_barrier(term.astype(jnp.bfloat16))
    return narrow.astype(jnp.float32)


def reference(tokens, routes, logits, grad_out, w_gate, w_up, w_down):
    total = tokens.shape[0]
    width = tokens.shape[1]
    blocks = N_DP * N_TENSOR
    span = w_gate.shape[2] // blocks
    most = EXPERTS * CAP
    contract_last = (((1,), (1,)), ((), ()))
    share = jax.nn.sigmoid(logits[:, 0] - logits[:, 1])
    weights = jnp.stack([share, 1.0 - share], axis=1).reshape(-1)
    flat = routes.reshape(-1).astype(jnp.int32)
    owner = jnp.arange(2 * total, dtype=jnp.int32) // 2
    order = jnp.argsort(flat, stable=True).astype(jnp.int32)
    order = jnp.concatenate([order, jnp.zeros((most,), jnp.int32)])
    labels = jnp.arange(EXPERTS, dtype=jnp.int32)
    counts = jnp.sum((flat[:, None] == labels[None, :]).astype(jnp.int32), axis=0)
    starts = (jnp.cumsum(counts) - counts).astype(jnp.int32)
    grad_rows = (weights[:, None] * grad_out[owner].astype(jnp.float32)).astype(jnp.bfloat16)
    positions = []
    valid = []
    expert_rows = []
    expert_backs = []
    for expert in range(EXPERTS):
        place = lax.dynamic_slice_in_dim(order, starts[expert], most, 0)
        positions.append(place)
        valid.append((jnp.arange(most, dtype=jnp.int32) < counts[expert])[:, None])
        expert_rows.append(tokens[owner[place]])
        expert_backs.append(grad_rows[place])

    def block_step(index, carry):
        out_total, back_total = carry
        out_terms = jnp.zeros((2 * total, width), jnp.float32)
        back_terms = jnp.zeros((2 * total, width), jnp.float32)
        for expert in range(EXPERTS):
            cols_gate = lax.dynamic_slice_in_dim(w_gate[expert], index * span, span, 1)
            cols_up = lax.dynamic_slice_in_dim(w_up[expert], index * span, span, 1)
            rows_down = lax.dynamic_slice_in_dim(w_down[expert], index * span, span, 0)
            gate = jnp.dot(expert_rows[expert], cols_gate, preferred_element_type=jnp.float32)
            up = jnp.dot(expert_rows[expert], cols_up, preferred_element_type=jnp.float32)
            hidden = activate(gate, up)
            term = round_term(jnp.dot(hidden, rows_down, preferred_element_type=jnp.float32))
            out_terms = out_terms.at[positions[expert]].add(jnp.where(valid[expert], term, 0.0))
            grad_hidden = lax.dot_general(expert_backs[expert], rows_down, contract_last, preferred_element_type=jnp.float32)
            grad_gate, grad_up = backprop(grad_hidden, gate, up)
            term_back = lax.dot_general(grad_gate, cols_gate, contract_last, preferred_element_type=jnp.float32)
            term_back = term_back + lax.dot_general(grad_up, cols_up, contract_last, preferred_element_type=jnp.float32)
            back_terms = back_terms.at[positions[expert]].add(jnp.where(valid[expert], round_term(term_back), 0.0))
        pairs = out_terms.reshape(total, 2, width)
        mixed = round_term(share[:, None] * pairs[:, 0] + (1.0 - share)[:, None] * pairs[:, 1])
        back_pairs = back_terms.reshape(total, 2, width)
        summed = round_term(back_pairs[:, 0] + back_pairs[:, 1])
        return out_total + mixed, back_total + summed

    zero = jnp.zeros((total, width), jnp.float32)
    out_total, back_total = lax.fori_loop(0, blocks, block_step, (zero, zero))
    return out_total.astype(jnp.bfloat16), back_total.astype(jnp.bfloat16)
```

```python
import functools

import jax
import jax.numpy as jnp
from jax import lax
from jax.experimental import pallas as pl
from jax.experimental.pallas import tpu as pltpu
from jax.sharding import PartitionSpec as P

INTERPRET = False
NN = (((1,), (0,)), ((), ()))
NT = (((1,), (1,)), ((), ()))
ORDER = (0, -1, 1, 2)


def shift_dp(value, step):
    return lax.ppermute(value, "dp", [(i, (i + step) % 4) for i in range(4)])


def shift_row(value, step):
    return lax.ppermute(
        value, "tensor", [(i, (i // 2 + step) % 4 * 2 + i % 2) for i in range(8)]
    )


def shift_expert(value, step):
    return lax.ppermute(value, "expert", [(i, (i + step) % 8) for i in range(8)])


def swap_core(value):
    return lax.ppermute(value, "tensor", [(i, i ^ 1) for i in range(8)])


def contract(indices, blocks, weights, down, start):
    count, rows, chunk = blocks.shape
    units = weights[0].shape[0 if down else 1]
    total = units * len(weights)

    def body(_, block, *refs):
        out = refs[-1]
        begin = refs[-2] if start is not None else None
        for i in range(len(weights)):
            part = lax.dot_general(
                block[0], refs[i][...], NT if down else NN, preferred_element_type=jnp.float32
            )
            place = pl.ds(i * units, units)

            @pl.when(pl.program_id(0) == 0)
            def _():
                out[:, place] = part if begin is None else part + begin[:, place]

            @pl.when(pl.program_id(0) > 0)
            def _():
                out[:, place] += part

    if down:
        weight_spec = pl.BlockSpec((units, chunk), lambda i, at: (0, at[i]))
    else:
        weight_spec = pl.BlockSpec((chunk, units), lambda i, at: (at[i], 0))
    total_spec = pl.BlockSpec((rows, total), lambda i, at: (0, 0))
    in_specs = [pl.BlockSpec((1, rows, chunk), lambda i, at: (i, 0, 0))]
    in_specs += [weight_spec] * len(weights)
    operands = [blocks, *weights]
    if start is not None:
        in_specs.append(total_spec)
        operands.append(start)
    return pl.pallas_call(
        body,
        grid_spec=pltpu.PrefetchScalarGridSpec(
            num_scalar_prefetch=1, grid=(count,), in_specs=in_specs, out_specs=total_spec
        ),
        out_shape=jax.ShapeDtypeStruct((rows, total), jnp.float32),
        interpret=INTERPRET,
        name="contract",
    )(indices, *operands)


def expand(indices, lefts, weights, chunk, down, groups):
    rows, units = lefts[0].shape
    count = 2 * groups

    def body(_, *refs):
        total = 0.0
        for k in range(len(lefts)):
            total = total + lax.dot_general(
                refs[k][...],
                refs[len(lefts) + k][...],
                NN if down else NT,
                preferred_element_type=jnp.float32,
            )
        total = total.astype(jnp.bfloat16)
        for j in range(groups):

            @pl.when(pl.program_id(0) // 2 == j)
            def _():
                refs[2 * len(lefts) + j][0] = total

    if down:
        weight_spec = pl.BlockSpec((units, chunk), lambda i, at: (0, at[i]))
    else:
        weight_spec = pl.BlockSpec((chunk, units), lambda i, at: (at[i], 0))
    left_spec = pl.BlockSpec((rows, units), lambda i, at: (0, 0))

    def out_spec(j):
        return pl.BlockSpec(
            (1, rows, chunk), lambda i, at: (jnp.minimum(jnp.maximum(i - 2 * j, 0), 1), 0, 0)
        )

    return pl.pallas_call(
        body,
        grid_spec=pltpu.PrefetchScalarGridSpec(
            num_scalar_prefetch=1,
            grid=(count,),
            in_specs=[left_spec] * len(lefts) + [weight_spec] * len(weights),
            out_specs=[out_spec(j) for j in range(groups)],
        ),
        out_shape=[jax.ShapeDtypeStruct((2, rows, chunk), jnp.bfloat16)] * groups,
        interpret=INTERPRET,
        name="expand",
    )(indices, *lefts, *weights)


def gather_ring(block, move):
    half = block.shape[0] // 2
    left = move(block, 1)
    right = move(block, -1)
    far_first = move(left[:half], 1)
    far_second = move(right[half:], -1)
    return left, right, far_first, far_second


def add(*values):
    total = values[0].astype(jnp.float32)
    for value in values[1:]:
        total = total + value.astype(jnp.float32)
    return total.astype(jnp.bfloat16)


def reduce_ring(own, left, right, far, move):
    first = move(far[0], 1)
    second = move(far[1], -1)
    right_b = move(right[1], 1)
    left_a = move(left[0], -1)
    right_a = move(add(right[0], first), 1)
    left_b = move(add(left[1], second), -1)
    return add(own[0], right_a, left_a), add(own[1], right_b, left_b)


def local(tokens, routes, logits, grad_out, w_gate, w_up, w_down):
    count, width = tokens.shape
    lanes = 16
    chunk = width // lanes
    capacity = 64
    half = capacity // 2
    x = lax.axis_index("dp")
    tensor = lax.axis_index("tensor")
    y = tensor // 2
    core = tensor % 2
    plane = lax.axis_index("expert")
    gate_own, up_own, down_own = w_gate[0], w_up[0], w_down[0]
    gate_far, up_far, down_far = swap_core(gate_own), swap_core(up_own), swap_core(down_own)

    flat = routes.reshape(-1)
    labels = jnp.arange(8, dtype=jnp.int32)
    onehot = (flat[:, None] == labels[None, :]).astype(jnp.int32)
    before = jnp.cumsum(onehot, axis=0) - onehot
    slot = jnp.sum(before * onehot, axis=1)
    target = (flat - plane) % 8 * half + slot % half
    target = jnp.where(slot // half == core, target, -1).reshape(-1, 2)
    share = jax.nn.sigmoid(logits[:, 0] - logits[:, 1])[:, None]
    rows = 8 * half
    places = jnp.arange(rows, dtype=jnp.int32)
    first = (places[:, None] == target[None, :, 0]).astype(jnp.bfloat16)
    second = (places[:, None] == target[None, :, 1]).astype(jnp.bfloat16)

    column = (x * 4 + y) * chunk
    token_part = lax.dynamic_slice(tokens, (0, column), (count, chunk))
    grad_part = lax.dynamic_slice(grad_out, (0, column), (count, chunk)).astype(jnp.float32)
    grad_one = (share * grad_part).astype(jnp.bfloat16)
    grad_two = ((1.0 - share) * grad_part).astype(jnp.bfloat16)
    built_fwd = jnp.dot(first + second, token_part, preferred_element_type=jnp.float32)
    built_bwd = jnp.dot(first, grad_one, preferred_element_type=jnp.float32)
    built_bwd = built_bwd + jnp.dot(second, grad_two, preferred_element_type=jnp.float32)
    built = jnp.concatenate(
        [
            built_fwd.astype(jnp.bfloat16).reshape(8, half, chunk),
            built_bwd.astype(jnp.bfloat16).reshape(8, half, chunk),
        ],
        axis=1,
    )
    arrived = [built[0]] + [shift_expert(built[k], k) for k in range(1, 8)]
    fwd = jnp.concatenate([piece[:half] for piece in arrived], axis=0)
    bwd = jnp.concatenate([piece[half:] for piece in arrived], axis=0)

    def chunk_at(dx, dy):
        return (x + dx) % 4 * 4 + (y + dy) % 4

    def many(pairs):
        return jnp.stack([chunk_at(dx, dy) for dx, dy in pairs]).astype(jnp.int32)

    gate_up = (gate_own, gate_far, up_own, up_far)
    downs = (down_own, down_far)

    def gather_plane(block, near, wide, weights, down, by_x):
        left, right, far_first, far_second = gather_ring(block, near)
        line = jnp.stack([block, left, right, jnp.concatenate([far_first, far_second], axis=0)])

        def at(step, others):
            return many([(step, o) if by_x else (o, step) for o in others])

        left, right, far_first, far_second = gather_ring(line, wide)
        total = contract(at(0, ORDER), line, weights, down, None)
        total = contract(at(-1, ORDER), left, weights, down, total)
        total = contract(at(1, ORDER), right, weights, down, total)
        total = contract(at(2, ORDER[:2]), far_first, weights, down, total)
        return contract(at(2, ORDER[2:]), far_second, weights, down, total)

    projected = gather_plane(fwd, shift_row, shift_dp, gate_up, False, True)
    grad_hidden = gather_plane(bwd, shift_dp, shift_row, downs, True, False)
    inner = gate_own.shape[1]
    gate = projected[:, : 2 * inner]
    up = projected[:, 2 * inner :]
    sig = jax.nn.sigmoid(gate)
    hidden = (gate * sig * up).astype(jnp.bfloat16)
    grad_gate = (grad_hidden * up * sig * (1.0 + gate * (1.0 - sig))).astype(jnp.bfloat16)
    grad_up = (grad_hidden * gate * sig).astype(jnp.bfloat16)

    def scatter_plane(lefts, weights, down, wide, near, by_x):
        def made(steps):
            pairs = [(s, o) if by_x else (o, s) for s in steps for o in ORDER]
            return expand(many(pairs), lefts, weights, chunk, down, 2 * len(steps))

        far = made((2,))
        sides = made((-1, 1))
        own = made((0,))
        a, b = reduce_ring(own, sides[:2], sides[2:], far, wide)
        mid = rows // 2

        def halves(value):
            return value[:mid], value[mid:]

        a, b = reduce_ring(halves(a[0]), halves(a[1]), halves(b[0]), halves(b[1]), near)
        return jnp.concatenate([a, b], axis=0).reshape(8, half, chunk)

    left_out = (hidden[:, :inner], hidden[:, inner:])
    left_back = (grad_gate[:, :inner], grad_gate[:, inner:], grad_up[:, :inner], grad_up[:, inner:])
    out_rows = scatter_plane(left_out, downs, True, shift_dp, shift_row, True)
    back_rows = scatter_plane(left_back, gate_up, False, shift_row, shift_dp, False)

    own_rows = count // 8

    def settle(summed, weight_one, weight_two):
        pieces = [summed[0]] + [shift_expert(summed[k], -k) for k in range(1, 8)]
        home = jnp.concatenate(pieces, axis=0)
        contract_first = (((0,), (0,)), ((), ()))
        one = lax.dot_general(first, home, contract_first, preferred_element_type=jnp.float32)
        two = lax.dot_general(second, home, contract_first, preferred_element_type=jnp.float32)
        mixed = (weight_one * one + weight_two * two).reshape(4, 2, own_rows, chunk)
        keep = jnp.where(core == 0, mixed[:, 0], mixed[:, 1])
        give = jnp.where(core == 0, mixed[:, 1], mixed[:, 0]).astype(jnp.bfloat16)
        done = (keep + swap_core(give).astype(jnp.float32)).astype(jnp.bfloat16)
        turned = [lax.dynamic_index_in_dim(done, (y + k) % 4, 0, keepdims=False) for k in range(4)]
        got = [turned[0]] + [shift_row(turned[k], k) for k in range(1, 4)]
        stacked = jnp.stack(got)
        line = jnp.concatenate(
            [lax.dynamic_index_in_dim(stacked, (y - v) % 4, 0, keepdims=False) for v in range(4)],
            axis=1,
        )
        lines = jnp.stack([line] + [shift_dp(line, k) for k in range(1, 4)])
        return jnp.concatenate(
            [lax.dynamic_index_in_dim(lines, (x - u) % 4, 0, keepdims=False) for u in range(4)],
            axis=1,
        )

    return settle(out_rows, share, 1.0 - share), settle(back_rows, 1.0, 1.0)


def solution(mesh):
    return jax.shard_map(
        local,
        mesh=mesh,
        in_specs=(
            P("expert", None),
            P("expert", None),
            P("expert", None),
            P("expert", None),
            P("expert", None, ("dp", "tensor")),
            P("expert", None, ("dp", "tensor")),
            P("expert", ("dp", "tensor"), None),
        ),
        out_specs=(P(("expert", "tensor"), None), P(("expert", "tensor"), None)),
        check_vma=False,
    )
```

```python
import jax
import jax.numpy as jnp
from jax import lax
from jax.experimental import pallas as pl
from jax.experimental.pallas import tpu as pltpu
from jax.sharding import PartitionSpec as P

INTERPRET = False
NN = (((1,), (0,)), ((), ()))
NT = (((1,), (1,)), ((), ()))
F32 = jnp.float32
BF16 = jnp.bfloat16
ANY = pl.BlockSpec(memory_space=pl.ANY)
WHOLE = pl.BlockSpec(memory_space=pltpu.VMEM)
SCALARS = pl.BlockSpec(memory_space=pltpu.SMEM)
PARAMS = pltpu.CompilerParams(vmem_limit_bytes=24 * 1024 * 1024)


def shift_dp(value, step):
    return lax.ppermute(value, "dp", [(i, (i + step) % 4) for i in range(4)])


def shift_row(value, step):
    return lax.ppermute(
        value, "tensor", [(i, (i // 2 + step) % 4 * 2 + i % 2) for i in range(8)]
    )


def swap_core(value):
    return lax.ppermute(value, "tensor", [(i, i ^ 1) for i in range(8)])


def exchange(value):
    return lax.all_to_all(value, "expert", split_axis=0, concat_axis=0, tiled=True)


def call(body, name, in_specs, out_shape, scratch, operands):
    out_specs = jax.tree.map(lambda _: WHOLE, out_shape)
    return pl.pallas_call(
        body,
        in_specs=in_specs,
        out_specs=out_specs,
        out_shape=out_shape,
        scratch_shapes=scratch,
        compiler_params=PARAMS,
        interpret=INTERPRET,
        name=name,
    )(*operands)


def part_of(weight, group, down):
    if down:
        size = weight.shape[1] // 4
        return weight.at[:, pl.ds(pl.multiple_of(group * size, size), size)]
    size = weight.shape[0] // 4
    return weight.at[pl.ds(pl.multiple_of(group * size, size), size), :]


def arrange(index, blocks):
    rows, chunk = blocks[0][0].shape

    def body(at, *refs):
        for j, distance in enumerate((0, -1, 1, 2)):
            place = pl.multiple_of((at[0] + distance + 4) % 4 * chunk, 128)
            for h in range(2):
                refs[8 + h][:, pl.ds(place, chunk)] = refs[2 * j + h][...]

    shape = jax.ShapeDtypeStruct((rows, 4 * chunk), BF16)
    flat = [half for pair in blocks for half in pair]
    return call(body, "arrange", [SCALARS] + [WHOLE] * 8, [shape] * 2, [], (index, *flat))


def load_rows(pairs, store, sems, base):
    half = pairs[0].shape[0]
    copies = []
    for j in range(len(pairs) // 2):
        for h in range(2):
            copy = pltpu.make_async_copy(
                pairs[2 * j + h], store.at[j, pl.ds(h * half, half)], sems.at[base + 2 * j + h]
            )
            copy.start()
            copies.append(copy)
    return copies


def contract(groups, pairs, weights, down, start):
    n, k = len(pairs), len(weights)
    half, size = pairs[0][0].shape
    units = weights[0].shape[0 if down else 1]
    begun = start is not None

    def body(*refs):
        at = refs[0]
        rows = refs[1 : 1 + 2 * n]
        sides = refs[1 + 2 * n : 1 + 2 * n + k]
        begin = refs[1 + 2 * n + k] if begun else None
        out, store, hold, row_sems, sems = refs[-5:]
        copies = load_rows(rows, store, row_sems, 0)
        for j in range(n):
            for i in range(k):
                pltpu.make_async_copy(
                    part_of(sides[i], at[j], down), hold.at[j * k + i], sems.at[j * k + i]
                ).start()
        for copy in copies:
            copy.wait()
        for j in range(n):

            def step(i, carry):
                slot = j * k + i
                pltpu.make_async_copy(
                    part_of(sides[0], at[j], down), hold.at[slot], sems.at[slot]
                ).wait()
                total = lax.dot_general(
                    store[j], hold[slot], NT if down else NN, preferred_element_type=F32
                )
                if j > 0:
                    out[i] += total
                elif begun:
                    out[i] = begin[i] + total
                else:
                    out[i] = total
                return carry

            lax.fori_loop(0, k, step, 0)

    operands = [groups, *[h for pair in pairs for h in pair], *weights]
    specs = [SCALARS] + [ANY] * (2 * n + k)
    if begun:
        operands.append(start)
        specs.append(WHOLE)
    piece = (units, size) if down else (size, units)
    return call(
        body,
        "contract",
        specs,
        jax.ShapeDtypeStruct((k, 2 * half, units), F32),
        [
            pltpu.VMEM((n, 2 * half, size), BF16),
            pltpu.VMEM((n * k, *piece), BF16),
            pltpu.SemaphoreType.DMA((2 * n,)),
            pltpu.SemaphoreType.DMA((n * k,)),
        ],
        operands,
    )


def finish(groups, fwd, bwd, gate_up, downs, total_fwd, total_bwd):
    half, size = fwd[0].shape
    units = downs[0].shape[0]
    rows = 2 * half

    def body(at, fa, fb, ba, bb, w0, w1, w2, w3, d0, d1, begin_f, begin_b, hidden, grads, *rest):
        store, hold, hold_d, total_f, total_b, row_sems, sems = rest
        copies = load_rows((fa, fb, ba, bb), store, row_sems, 0)
        for i, weight in enumerate((w0, w1, w2, w3)):
            pltpu.make_async_copy(
                part_of(weight, at[0], False), hold.at[i], sems.at[i]
            ).start()
        for i, weight in enumerate((d0, d1)):
            pltpu.make_async_copy(
                part_of(weight, at[1], True), hold_d.at[i], sems.at[4 + i]
            ).start()
        for copy in copies:
            copy.wait()

        def step_f(i, carry):
            pltpu.make_async_copy(part_of(w0, at[0], False), hold.at[i], sems.at[i]).wait()
            total_f[i] = begin_f[i] + lax.dot_general(
                store[0], hold[i], NN, preferred_element_type=F32
            )
            return carry

        def step_b(i, carry):
            pltpu.make_async_copy(part_of(d0, at[1], True), hold_d.at[i], sems.at[4 + i]).wait()
            total_b[i] = begin_b[i] + lax.dot_general(
                store[1], hold_d[i], NT, preferred_element_type=F32
            )
            return carry

        lax.fori_loop(0, 4, step_f, 0)
        lax.fori_loop(0, 2, step_b, 0)

        def act(t, carry):
            part = pl.ds(t * (rows // 8), rows // 8)
            for i in range(2):
                gate = total_f[i, part]
                up = total_f[2 + i, part]
                grad = total_b[i, part]
                sig = jax.nn.sigmoid(gate)
                hidden[i, part] = (gate * sig * up).astype(BF16)
                slope = sig * (1.0 + gate * (1.0 - sig))
                grads[i, part] = (grad * up * slope).astype(BF16)
                grads[2 + i, part] = (grad * gate * sig).astype(BF16)
            return carry

        lax.fori_loop(0, 8, act, 0)

    return call(
        body,
        "finish",
        [SCALARS] + [ANY] * 10 + [WHOLE] * 2,
        [
            jax.ShapeDtypeStruct((2, rows, units), BF16),
            jax.ShapeDtypeStruct((4, rows, units), BF16),
        ],
        [
            pltpu.VMEM((2, rows, size), BF16),
            pltpu.VMEM((4, size, units), BF16),
            pltpu.VMEM((2, units, size), BF16),
            pltpu.VMEM((4, rows, units), F32),
            pltpu.VMEM((2, rows, units), F32),
            pltpu.SemaphoreType.DMA((4,)),
            pltpu.SemaphoreType.DMA((6,)),
        ],
        (groups, *fwd, *bwd, *gate_up, *downs, total_fwd, total_bwd),
    )


def expand(groups, n, lefts, weights, down):
    k = len(weights)
    rows, units = lefts.shape[1:]
    size = weights[0].shape[1 if down else 0] // 4
    half = rows // 2
    tiles = 3
    width = size // tiles

    def body(*refs):
        at, left = refs[:2]
        sides = refs[2 : 2 + k]
        outs = refs[2 + k : 2 + k + 2 * n]
        hold, sems = refs[-2:]
        for j in range(n):
            for i in range(k):
                pltpu.make_async_copy(
                    part_of(sides[i], at[j], down), hold.at[j * k + i], sems.at[j * k + i]
                ).start()
        for j in range(n):
            for i in range(k):
                pltpu.make_async_copy(
                    part_of(sides[i], at[j], down), hold.at[j * k + i], sems.at[j * k + i]
                ).wait()

            def step(t, carry):
                place = pl.ds(pl.multiple_of(t * width, 128), width)
                total = 0.0
                for i in range(k):
                    side = hold[j * k + i, :, place] if down else hold[j * k + i, place, :]
                    total = total + lax.dot_general(
                        left[i], side, NN if down else NT, preferred_element_type=F32
                    )
                outs[2 * j][:, place] = total[:half].astype(BF16)
                outs[2 * j + 1][:, place] = total[half:].astype(BF16)
                return carry

            lax.fori_loop(0, tiles, step, 0)

    piece = (units, size) if down else (size, units)
    return call(
        body,
        "expand",
        [SCALARS, WHOLE] + [ANY] * k,
        [jax.ShapeDtypeStruct((half, size), BF16)] * (2 * n),
        [pltpu.VMEM((n * k, *piece), BF16), pltpu.SemaphoreType.DMA((n * k,))],
        (groups, lefts, *weights),
    )


def part_sums(index, values):
    half, size = values[0].shape
    chunk = size // 4

    def body(at, *refs):
        outs = refs[6:]
        for j, distance in enumerate((0, -1, 1, 2)):
            place = pl.ds(pl.multiple_of((at[0] + distance + 4) % 4 * chunk, 128), chunk)
            for h in range(2):
                total = refs[h][:, place].astype(F32) + refs[2 + h][:, place].astype(F32)
                total = total + refs[4 + h][:, place].astype(F32)
                outs[2 * j + h][...] = total.astype(BF16)

    shape = jax.ShapeDtypeStruct((half, chunk), BF16)
    flat = call(body, "part_sums", [SCALARS] + [WHOLE] * 6, [shape] * 8, [], (index, *values))
    return [flat[2 * j : 2 * j + 2] for j in range(4)]


def last_sums(first, second, planes, slots):
    half, chunk = first[0].shape
    per = half // slots

    def body(*refs):
        out = refs[12]
        for a in range(2):
            for h in range(2):
                total = refs[6 * a + h][...].astype(F32) + refs[6 * a + 2 + h][...].astype(F32)
                total = (total + refs[6 * a + 4 + h][...].astype(F32)).astype(BF16)
                for s in range(per):
                    out[h * per + s, pl.ds(a * slots, slots), :] = total[
                        s * slots : (s + 1) * slots
                    ]

    return call(
        body,
        "last_sums",
        [WHOLE] * 12,
        jax.ShapeDtypeStruct((planes, 2 * slots, chunk), BF16),
        [],
        (*first, *second),
    )


def combine(target, share, home):
    count = target.shape[0]
    planes, both, chunk = home.shape
    slots = both // 2
    group = count // 8

    def body(target_ref, share_ref, home_ref, keep, give):
        places = lax.broadcasted_iota(jnp.int32, (count, planes * slots), 1)
        first = jnp.where(places == target_ref[:, 0:1], 1.0, 0.0).astype(BF16)
        second = jnp.where(places == target_ref[:, 1:2], 1.0, 0.0).astype(BF16)
        weight = share_ref[...]
        for a in range(2):
            rows = jnp.concatenate(
                [home_ref[s, pl.ds(a * slots, slots), :] for s in range(planes)], axis=0
            )
            one = lax.dot_general(first, rows, NN, preferred_element_type=F32)
            two = lax.dot_general(second, rows, NN, preferred_element_type=F32)
            mixed = weight * one + (1.0 - weight) * two if a == 0 else one + two
            mixed = mixed.astype(BF16)
            for v in range(4):
                place = pl.ds(a * group, group)
                keep[v, place, :] = mixed[v * group : (v + 1) * group]
                give[v, place, :] = mixed[(4 + v) * group : (5 + v) * group]

    shape = jax.ShapeDtypeStruct((4, 2 * group, chunk), BF16)
    return call(body, "combine", [WHOLE] * 3, [shape] * 2, [], (target, share, home))


def add_cores(keep, other):
    def body(keep_ref, other_ref, *outs):
        for v in range(4):
            total = keep_ref[v].astype(F32) + other_ref[v].astype(F32)
            outs[v][...] = total.astype(BF16)

    shape = jax.ShapeDtypeStruct(keep.shape[1:], BF16)
    return call(body, "add_cores", [WHOLE] * 2, [shape] * 4, [], (keep, other))


def place(index, lines):
    _, both, chunk = lines[0].shape
    group = both // 2

    def body(at, *refs):
        out, grad = refs[4:]
        for k in range(4):
            for j in range(4):
                xs = (at[0] - k + 4) % 4
                ys = (at[1] - j + 4) % 4
                one = pl.ds(pl.multiple_of((xs * 4 + ys) * chunk, 128), chunk)
                two = pl.ds(pl.multiple_of((ys * 4 + xs) * chunk, 128), chunk)
                out[:, one] = refs[k][j, :group, :]
                grad[:, two] = refs[k][j, group:, :]

    shape = jax.ShapeDtypeStruct((group, 16 * chunk), BF16)
    return call(body, "place", [SCALARS] + [WHOLE] * 4, [shape] * 2, [], (index, *lines))


def gather_ring(pair, move):
    a, b = pair
    left_a = move(a, 1)
    right_b = move(b, -1)
    left_b = move(b, 1)
    right_a = move(a, -1)
    far_a = move(left_a, 1)
    far_b = move(right_b, -1)
    return pair, (left_a, left_b), (right_a, right_b), (far_a, far_b)


def add(one, two):
    return (one.astype(F32) + two.astype(F32)).astype(BF16)


def reduce_ring(own, left, right, far, move):
    first = move(far[0], 1)
    second = move(far[1], -1)
    right_b = move(right[1], 1)
    left_a = move(left[0], -1)
    right_a = move(add(right[0], first), 1)
    left_b = move(add(left[1], second), -1)
    return (*own, right_a, right_b, left_a, left_b)


def local(tokens, routes, logits, grad_out, w_gate, w_up, w_down):
    count, width = tokens.shape
    chunk = width // 16
    capacity = 64
    half = capacity // 2
    x = lax.axis_index("dp")
    tensor = lax.axis_index("tensor")
    y = tensor // 2
    core = tensor % 2

    def scalars(*values):
        return jnp.stack([value % 4 for value in values]).astype(jnp.int32)

    flat = routes.reshape(-1)
    labels = jnp.arange(8, dtype=jnp.int32)
    onehot = (flat[:, None] == labels[None, :]).astype(jnp.int32)
    before = jnp.cumsum(onehot, axis=0) - onehot
    slot = jnp.sum(before * onehot, axis=1)
    target = jnp.where(slot // half == core, flat * half + slot % half, -1).reshape(-1, 2)
    share = jax.nn.sigmoid(logits[:, 0] - logits[:, 1])[:, None]
    rows = 8 * half
    places = jnp.arange(rows, dtype=jnp.int32)
    first = (places[:, None] == target[None, :, 0]).astype(BF16)
    second = (places[:, None] == target[None, :, 1]).astype(BF16)

    token_part = lax.dynamic_slice(tokens, (0, (x * 4 + y) * chunk), (count, chunk))
    grad_part = lax.dynamic_slice(grad_out, (0, (y * 4 + x) * chunk), (count, chunk)).astype(F32)
    grad_one = (share * grad_part).astype(BF16)
    grad_two = ((1.0 - share) * grad_part).astype(BF16)
    built_fwd = jnp.dot(first + second, token_part, preferred_element_type=F32)
    built_bwd = jnp.dot(first, grad_one, preferred_element_type=F32)
    built_bwd = built_bwd + jnp.dot(second, grad_two, preferred_element_type=F32)
    built = jnp.concatenate(
        [
            built_fwd.astype(BF16).reshape(8, half, chunk),
            built_bwd.astype(BF16).reshape(8, half, chunk),
        ],
        axis=1,
    )
    arrived = exchange(built)

    def halves(value):
        return value[:4].reshape(rows // 2, chunk), value[4:].reshape(rows // 2, chunk)

    own = (w_gate[0], w_up[0], w_down[0])
    far = [swap_core(weight) for weight in own]
    gate_up = (own[0], far[0], own[1], far[1])
    downs = (own[2], far[2])

    fwd_line = arrange(scalars(y), gather_ring(halves(arrived[:, :half]), shift_row))
    bwd_line = arrange(scalars(x), gather_ring(halves(arrived[:, half:]), shift_dp))
    fwd = gather_ring(fwd_line, shift_dp)
    bwd = gather_ring(bwd_line, shift_row)
    total_fwd = contract(scalars(x), fwd[:1], gate_up, False, None)
    total_bwd = contract(scalars(y), bwd[:1], downs, True, None)
    total_fwd = contract(scalars(x - 1, x + 1), fwd[1:3], gate_up, False, total_fwd)
    total_bwd = contract(scalars(y - 1, y + 1), bwd[1:3], downs, True, total_bwd)
    hidden, grads = finish(
        scalars(x + 2, y + 2), fwd[3], bwd[3], gate_up, downs, total_fwd, total_bwd
    )

    def scatter_plane(at, near_at, lefts, weights, down, wide, near):
        far = expand(scalars(at + 2), 1, lefts, weights, down)
        sides = expand(scalars(at - 1, at + 1), 2, lefts, weights, down)
        mine = expand(scalars(at), 1, lefts, weights, down)
        got = reduce_ring(mine, sides[:2], sides[2:], far, wide)
        return reduce_ring(*part_sums(scalars(near_at), got), near)

    out_parts = scatter_plane(x, y, hidden, downs, True, shift_dp, shift_row)
    back_parts = scatter_plane(y, x, grads, gate_up, False, shift_row, shift_dp)
    home = exchange(last_sums(out_parts, back_parts, 8, half))

    group = count // 8
    order = jnp.arange(4, dtype=jnp.int32)[:, None] * 0 + (
        (y + jnp.arange(4, dtype=jnp.int32)[:, None]) % 4 * 2 * group
        + jnp.arange(group, dtype=jnp.int32)[None, :]
    )
    order = jnp.concatenate([order + core * group, order + (1 - core) * group]).reshape(-1)
    keep, give = combine(target[order], share[order], home)
    done = add_cores(keep, swap_core(give))
    line = jnp.stack([done[0]] + [shift_row(done[k], k) for k in range(1, 4)])
    lines = [line] + [shift_dp(line, k) for k in range(1, 4)]
    output, grad_tokens = place(scalars(x, y), lines)
    return output, grad_tokens


def solution(mesh):
    return jax.shard_map(
        local,
        mesh=mesh,
        in_specs=(
            P("expert", None),
            P("expert", None),
            P("expert", None),
            P("expert", None),
            P("expert", None, ("dp", "tensor")),
            P("expert", None, ("dp", "tensor")),
            P("expert", ("dp", "tensor"), None),
        ),
        out_specs=(P(("expert", "tensor"), None), P(("expert", "tensor"), None)),
        check_vma=False,
    )
```

```python
import jax
import jax.numpy as jnp
from jax import lax
from jax.experimental import pallas as pl
from jax.experimental.pallas import tpu as pltpu
from jax.sharding import PartitionSpec as P


INTERPRET = False
NN = (((1,), (0,)), ((), ()))
NT = (((1,), (1,)), ((), ()))
F32 = jnp.float32
BF16 = jnp.bfloat16
ANY = pl.BlockSpec(memory_space=pl.ANY)
HBM = pl.BlockSpec(memory_space=pltpu.HBM)
WHOLE = pl.BlockSpec(memory_space=pltpu.VMEM)
SCALARS = pl.BlockSpec(memory_space=pltpu.SMEM)
MIB = 1024 * 1024


def shift_dp(value, step):
    return lax.ppermute(value, "dp", [(i, (i + step) % 4) for i in range(4)])


def shift_row(value, step):
    return lax.ppermute(
        value, "tensor", [(i, (i // 2 + step) % 4 * 2 + i % 2) for i in range(8)]
    )


def swap_core(value):
    return lax.ppermute(value, "tensor", [(i, i ^ 1) for i in range(8)])


def exchange(value):
    return lax.all_to_all(value, "expert", split_axis=0, concat_axis=0, tiled=True)


def call(body, in_specs, out_shape, scratch, operands, flops=0, moved=0, limit=24):
    out_specs = jax.tree.map(lambda _: WHOLE, out_shape)
    cost = pl.CostEstimate(flops=flops, bytes_accessed=moved, transcendentals=0) if flops else None
    return pl.pallas_call(
        body,
        in_specs=in_specs,
        out_specs=out_specs,
        out_shape=out_shape,
        scratch_shapes=scratch,
        compiler_params=pltpu.CompilerParams(vmem_limit_bytes=limit * MIB),
        cost_estimate=cost,
        interpret=INTERPRET,
    )(*operands)


def part_of(weight, group, down):
    if down:
        size = weight.shape[1] // 4
        return weight.at[:, pl.ds(pl.multiple_of(group * size, size), size)]
    size = weight.shape[0] // 4
    return weight.at[pl.ds(pl.multiple_of(group * size, size), size), :]


def prepare(at, routes, logits, tokens, grad_out, capacity):
    count, width = tokens.shape
    size = width // 4
    experts = 8
    half = capacity // 2
    quarter = half // 2
    tiles = 3
    part = size // tiles

    def body(at, route_ref, logit_ref, token_ref, grad_ref, out_a, out_b, target, weight, *rest):
        token_part, grad_part, sems = rest
        copies = []
        for i, (source, hold) in enumerate(((token_ref, token_part), (grad_ref, grad_part))):
            begin = pl.multiple_of(at[i] * size, 128)
            copy = pltpu.make_async_copy(source.at[:, pl.ds(begin, size)], hold, sems.at[i])
            copy.start()
            copies.append(copy)
        row = lax.broadcasted_iota(jnp.int32, (count, count), 0)
        column = lax.broadcasted_iota(jnp.int32, (count, count), 1)
        before = jnp.where(row > column, 1.0, 0.0).astype(BF16)
        names = [route_ref[:, j : j + 1] for j in range(2)]
        hots = [jnp.where(column == name, 1.0, 0.0) for name in names]
        passed = jnp.sum(hots[0], axis=0, keepdims=True)
        masks = []
        for j in range(2):
            earlier = lax.dot_general(before, hots[j].astype(BF16), NN, preferred_element_type=F32)
            if j == 1:
                earlier = earlier + passed
            slot = jnp.sum(earlier * hots[j], axis=1, keepdims=True).astype(jnp.int32)
            mine = slot // half == at[2]
            inner = slot % half
            target[:, j : j + 1] = jnp.where(mine, names[j] * half + inner, -1)
            spot = inner // quarter * (experts * quarter) + names[j] * quarter + inner % quarter
            spot = jnp.where(mine, spot, -1)
            line = jnp.sum(jnp.where(row == column, spot, 0), axis=0, keepdims=True)
            places = lax.broadcasted_iota(jnp.int32, (experts * half, count), 0)
            masks.append(jnp.where(places == line, 1.0, 0.0).astype(BF16))
        share = jax.nn.sigmoid(logit_ref[:, 0:1] - logit_ref[:, 1:2])
        weight[...] = share
        for copy in copies:
            copy.wait()

        def step(t, carry):
            place = pl.ds(pl.multiple_of(t * part, 128), part)
            fwd = lax.dot_general(
                masks[0] + masks[1], token_part[:, place], NN, preferred_element_type=F32
            )
            grad = grad_part[:, place].astype(F32)
            bwd = lax.dot_general(
                masks[0], (share * grad).astype(BF16), NN, preferred_element_type=F32
            )
            bwd = bwd + lax.dot_general(
                masks[1], ((1.0 - share) * grad).astype(BF16), NN, preferred_element_type=F32
            )
            fwd = fwd.astype(BF16).reshape(2, experts, quarter, part)
            bwd = bwd.astype(BF16).reshape(2, experts, quarter, part)
            for h, out in enumerate((out_a, out_b)):
                out[:, :quarter, place] = fwd[h]
                out[:, quarter:, place] = bwd[h]
            return carry

        lax.fori_loop(0, tiles, step, 0)

    built = jax.ShapeDtypeStruct((experts, half, size), BF16)
    return call(
        body,
        [SCALARS, WHOLE, WHOLE, HBM, HBM],
        [
            built,
            built,
            jax.ShapeDtypeStruct((count, 2), jnp.int32),
            jax.ShapeDtypeStruct((count, 1), F32),
        ],
        [
            pltpu.VMEM((count, size), BF16),
            pltpu.VMEM((count, size), BF16),
            pltpu.SemaphoreType.DMA((2,)),
        ],
        (at, routes, logits, tokens, grad_out),
        limit=58,
    )


def load_rows(pairs, store, sems, base):
    half = pairs[0].shape[0]
    copies = []
    for j in range(len(pairs) // 2):
        for h in range(2):
            copy = pltpu.make_async_copy(
                pairs[2 * j + h], store.at[j, pl.ds(h * half, half)], sems.at[base + 2 * j + h]
            )
            copy.start()
            copies.append(copy)
    return copies


def project(groups, fwd, bwd, gate_up, downs, starts, last):
    n = len(fwd)
    half, size = fwd[0][0].shape
    units = downs[0].shape[0]
    rows = 2 * half
    begun = starts is not None

    def body(*refs):
        at = refs[0]
        pairs = refs[1 : 1 + 4 * n]
        sides = refs[1 + 4 * n : 7 + 4 * n]
        begin = refs[7 + 4 * n : 9 + 4 * n] if begun else (None, None)
        if last:
            hidden, grads, store, hold, hold_d, *outs, row_sems, sems = refs[-9:]
        else:
            outs = refs[-7:-5]
            store, hold, hold_d, row_sems, sems = refs[-5:]
        copies = load_rows(pairs, store, row_sems, 0)

        def copy(which, j, i):
            source = sides[4 * which + i]
            target = (hold, hold_d)[which].at[j * (4, 2)[which] + i]
            sem = sems.at[which * 4 * n + j * (4, 2)[which] + i]
            part = part_of(source, at[which * n + j], which == 1)
            return pltpu.make_async_copy(part, target, sem)

        for which in range(2):
            for j in range(n):
                for i in range((4, 2)[which]):
                    copy(which, j, i).start()
        for each in copies:
            each.wait()
        for which in range(2):
            k = (4, 2)[which]
            out = outs[which]

            def step(t, carry):
                i = t % k
                pltpu.make_async_copy(
                    part_of(sides[4 * which], at[which * n], which == 1),
                    (hold, hold_d)[which].at[t],
                    sems.at[which * 4 * n + t],
                ).wait()
                total = lax.dot_general(
                    store[which * n + t // k],
                    (hold, hold_d)[which][t],
                    NT if which else NN,
                    preferred_element_type=F32,
                )

                @pl.when(t < k)
                def _():
                    out[i] = total + begin[which][i] if begun else total

                if n > 1:

                    @pl.when(t >= k)
                    def _():
                        out[i] += total

                return carry

            lax.fori_loop(0, n * k, step, 0)
        if not last:
            return

        def act(t, carry):
            part = pl.ds(t * (rows // 8), rows // 8)
            for i in range(2):
                gate = outs[0][i, part]
                up = outs[0][2 + i, part]
                grad = outs[1][i, part]
                sig = jax.nn.sigmoid(gate)
                hidden[i, part] = (gate * sig * up).astype(BF16)
                slope = sig * (1.0 + gate * (1.0 - sig))
                grads[i, part] = (grad * up * slope).astype(BF16)
                grads[2 + i, part] = (grad * gate * sig).astype(BF16)
            return carry

        lax.fori_loop(0, 8, act, 0)

    shapes = [(4, rows, units), (2, rows, units)]
    scratch = [
        pltpu.VMEM((2 * n, rows, size), BF16),
        pltpu.VMEM((4 * n, size, units), BF16),
        pltpu.VMEM((2 * n, units, size), BF16),
    ]
    if last:
        scratch += [pltpu.VMEM(shape, F32) for shape in shapes]
        out_shape = [
            jax.ShapeDtypeStruct((2, rows, units), BF16),
            jax.ShapeDtypeStruct((4, rows, units), BF16),
        ]
    else:
        out_shape = [jax.ShapeDtypeStruct(shape, F32) for shape in shapes]
    scratch += [pltpu.SemaphoreType.DMA((4 * n,)), pltpu.SemaphoreType.DMA((6 * n,))]
    operands = [groups, *[half for pair in (*fwd, *bwd) for half in pair], *gate_up, *downs]
    specs = [SCALARS] + [ANY] * (4 * n) + [HBM] * 6
    if begun:
        operands += list(starts)
        specs += [WHOLE] * 2
    return call(
        body,
        specs,
        out_shape,
        scratch,
        operands,
        flops=2 * rows * size * units * 6 * n,
        moved=2 * size * units * 6 * n,
        limit=24 if last else 56,
    )


def expand(groups, n, hidden, grads, gate_up, downs):
    rows, units = hidden.shape[1:]
    size = downs[0].shape[1] // 4
    half = rows // 2
    tiles = 3
    width = size // tiles

    def body(at, left_d, left_g, d0, d1, w0, w1, w2, w3, *rest):
        outs = rest[: 4 * n]
        hold_d, hold_g, sems = rest[4 * n :]
        sides = ((d0, d1), (w0, w1, w2, w3))

        def copy(which, j, i):
            down = which == 0
            hold = (hold_d, hold_g)[which]
            k = (2, 4)[which]
            return pltpu.make_async_copy(
                part_of(sides[which][i], at[which * n + j], down),
                hold.at[j * k + i],
                sems.at[which * 2 * n + j * k + i],
            )

        for which in range(2):
            for j in range(n):
                for i in range((2, 4)[which]):
                    copy(which, j, i).start()
        for which in range(2):
            k = (2, 4)[which]
            left = (left_d, left_g)[which]
            for j in range(n):
                for i in range(k):
                    copy(which, j, i).wait()

            def step(at_step, carry):
                j = at_step // tiles
                place = pl.ds(pl.multiple_of(at_step % tiles * width, 128), width)
                total = 0.0
                for i in range(k):
                    if which == 0:
                        side = hold_d[j * k + i, :, place]
                    else:
                        side = hold_g[j * k + i, place, :]
                    total = total + lax.dot_general(
                        left[i], side, NN if which == 0 else NT, preferred_element_type=F32
                    )
                for m in range(n):

                    @pl.when(j == m)
                    def _():
                        outs[which * 2 * n + 2 * m][:, place] = total[:half].astype(BF16)
                        outs[which * 2 * n + 2 * m + 1][:, place] = total[half:].astype(BF16)

                return carry

            lax.fori_loop(0, n * tiles, step, 0)

    flat = call(
        body,
        [SCALARS, WHOLE, WHOLE] + [HBM] * 6,
        [jax.ShapeDtypeStruct((half, size), BF16)] * (4 * n),
        [
            pltpu.VMEM((n * 2, units, size), BF16),
            pltpu.VMEM((n * 4, size, units), BF16),
            pltpu.SemaphoreType.DMA((n * 6,)),
        ],
        (groups, hidden, grads, *downs, *gate_up),
        flops=2 * rows * size * units * 6 * n,
        moved=2 * size * units * 6 * n,
    )
    return flat[: 2 * n], flat[2 * n :]


def part_sums(index, values):
    half, size = values[0].shape
    chunk = size // 4

    def body(at, *refs):
        outs = refs[6:]
        for j, distance in enumerate((0, -1, 1, 2)):
            place = pl.ds(pl.multiple_of((at[0] + distance + 4) % 4 * chunk, 128), chunk)
            for h in range(2):
                total = refs[h][:, place].astype(F32) + refs[2 + h][:, place].astype(F32)
                total = total + refs[4 + h][:, place].astype(F32)
                outs[j][h * half : (h + 1) * half, :] = total.astype(BF16)

    shape = jax.ShapeDtypeStruct((2 * half, chunk), BF16)
    return call(body, [SCALARS] + [WHOLE] * 6, [shape] * 4, [], (index, *values))


def last_sums(first, second, planes, slots):
    _, chunk = first[0].shape
    quarter = slots // 2

    def body(*refs):
        out = refs[8]
        for a in range(2):
            total = refs[4 * a][...].astype(F32)
            for i in range(1, 4):
                total = total + refs[4 * a + i][...].astype(F32)
            total = total.astype(BF16).reshape(2, planes, quarter, chunk)
            for h in range(2):
                place = pl.ds(a * slots + h * quarter, quarter)
                out[:, place, :] = total[h]

    return call(
        body,
        [WHOLE] * 8,
        jax.ShapeDtypeStruct((planes, 2 * slots, chunk), BF16),
        [],
        (*first, *second),
    )


def combine(target, share, home):
    count = target.shape[0]
    planes, both, chunk = home.shape
    slots = both // 2
    group = count // 8

    def body(target_ref, share_ref, home_ref, keep, give):
        places = lax.broadcasted_iota(jnp.int32, (count, planes * slots), 1)
        first = jnp.where(places == target_ref[:, 0:1], 1.0, 0.0).astype(BF16)
        second = jnp.where(places == target_ref[:, 1:2], 1.0, 0.0).astype(BF16)
        weight = share_ref[...]
        for a in range(2):
            rows = jnp.concatenate(
                [home_ref[s, pl.ds(a * slots, slots), :] for s in range(planes)], axis=0
            )
            one = lax.dot_general(first, rows, NN, preferred_element_type=F32)
            two = lax.dot_general(second, rows, NN, preferred_element_type=F32)
            mixed = weight * one + (1.0 - weight) * two if a == 0 else one + two
            mixed = mixed.astype(BF16)
            for v in range(4):
                place = pl.ds(a * group, group)
                keep[v, place, :] = mixed[v * group : (v + 1) * group]
                give[v, place, :] = mixed[(4 + v) * group : (5 + v) * group]

    shape = jax.ShapeDtypeStruct((4, 2 * group, chunk), BF16)
    return call(body, [WHOLE] * 3, [shape] * 2, [], (target, share, home))


def add_cores(keep, other):
    def body(keep_ref, other_ref, *outs):
        for v in range(4):
            total = keep_ref[v].astype(F32) + other_ref[v].astype(F32)
            outs[v][...] = total.astype(BF16)

    shape = jax.ShapeDtypeStruct(keep.shape[1:], BF16)
    return call(body, [WHOLE] * 2, [shape] * 4, [], (keep, other))


def place(index, lines):
    _, both, chunk = lines[0].shape
    group = both // 2

    def body(at, *refs):
        out, grad = refs[4:]
        for k in range(4):
            for j in range(4):
                xs = (at[0] - k + 4) % 4
                ys = (at[1] - j + 4) % 4
                one = pl.ds(pl.multiple_of((xs * 4 + ys) * chunk, 128), chunk)
                two = pl.ds(pl.multiple_of((ys * 4 + xs) * chunk, 128), chunk)
                out[:, one] = refs[k][j, :group, :]
                grad[:, two] = refs[k][j, group:, :]

    shape = jax.ShapeDtypeStruct((group, 16 * chunk), BF16)
    return call(body, [SCALARS] + [WHOLE] * 4, [shape] * 2, [], (index, *lines))


def gather_near(half, move):
    left = move(half, 1)
    return left, move(half, -1)


def add(one, two):
    return (one.astype(F32) + two.astype(F32)).astype(BF16)


def reduce_ring(own, left, right, far, move):
    first = move(far[0], 1)
    second = move(far[1], -1)
    right_b = move(right[1], 1)
    left_a = move(left[0], -1)
    right_a = move(add(right[0], first), 1)
    left_b = move(add(left[1], second), -1)
    return (*own, right_a, right_b, left_a, left_b)


def reorder(at, target, share):
    count = target.shape[0]
    group = count // 8

    def body(at_ref, target_ref, share_ref, target_out, share_out):
        for c in range(2):
            core = (at_ref[2] + c) % 2
            for v in range(4):
                start = ((at_ref[1] + v) % 4 * 2 + core) * group
                source = pl.ds(pl.multiple_of(start, group), group)
                place = pl.ds((c * 4 + v) * group, group)
                target_out[place, :] = target_ref[source, :]
                share_out[place, :] = share_ref[source, :]

    shapes = [
        jax.ShapeDtypeStruct((count, 2), jnp.int32),
        jax.ShapeDtypeStruct((count, 1), F32),
    ]
    return call(body, [SCALARS] + [WHOLE] * 2, shapes, [], (at, target, share))


def local(tokens, routes, logits, grad_out, w_gate, w_up, w_down):
    capacity = 64
    half = capacity // 2
    x = lax.axis_index("dp")
    tensor = lax.axis_index("tensor")
    y = tensor // 2
    core = tensor % 2

    def scalars(*values):
        return jnp.stack([value % 4 for value in values]).astype(jnp.int32)

    own = (w_gate[0], w_up[0], w_down[0])
    far = [swap_core(weight) for weight in own]
    gate_up = (own[0], far[0], own[1], far[1])
    downs = (own[2], far[2])

    at = jnp.stack([x, y, core]).astype(jnp.int32)
    built_a, built_b, target, share = prepare(at, routes, logits, tokens, grad_out, capacity)
    quarter = half // 2

    def rows_of(piece):
        return [p.reshape(8 * quarter, -1) for p in (piece[:, :quarter], piece[:, quarter:])]

    fwd_a, bwd_a = rows_of(exchange(built_a))
    fwd_b, bwd_b = rows_of(exchange(built_b))
    order = reorder(at, target, share)

    def gather(a, b, move):
        left_a, right_a = gather_near(a, move)
        far_a = move(left_a, 1)
        left_b, right_b = gather_near(b, move)
        far_b = move(right_b, -1)
        return (a, b), (left_a, left_b), (right_a, right_b), (far_a, far_b)

    fwd = gather(fwd_a, fwd_b, shift_dp)
    bwd = gather(bwd_a, bwd_b, shift_row)
    weights = (gate_up, downs)
    total = project(scalars(x, y), fwd[:1], bwd[:1], *weights, None, False)
    near = scalars(x - 1, x + 1, y - 1, y + 1)
    total = project(near, fwd[1:3], bwd[1:3], *weights, total, False)
    hidden, grads = project(scalars(x + 2, y + 2), fwd[3:], bwd[3:], *weights, total, True)

    sides = (hidden, grads, gate_up, downs)
    far_out, far_back = expand(scalars(x + 2, y + 2), 1, *sides)
    side_out, side_back = expand(near, 2, *sides)
    own_out, own_back = expand(scalars(x, y), 1, *sides)
    got_out = reduce_ring(own_out, side_out[:2], side_out[2:], far_out, shift_dp)
    got_back = reduce_ring(own_back, side_back[:2], side_back[2:], far_back, shift_row)

    def settle(parts, move):
        return parts[0], move(parts[3], 2), move(parts[1], -1), move(parts[2], 1)

    out_parts = settle(part_sums(scalars(y), got_out), shift_row)
    back_parts = settle(part_sums(scalars(x), got_back), shift_dp)
    home = exchange(last_sums(out_parts, back_parts, 8, half))

    keep, give = combine(*order, home)
    done = add_cores(keep, swap_core(give))
    line = jnp.stack([done[0]] + [shift_row(done[k], k) for k in range(1, 4)])
    lines = [line] + [shift_dp(line, k) for k in range(1, 4)]
    output, grad_tokens = place(scalars(x, y), lines)
    return output, grad_tokens


def solution(mesh):
    return jax.shard_map(
        local,
        mesh=mesh,
        in_specs=(
            P("expert", None),
            P("expert", None),
            P("expert", None),
            P("expert", None),
            P("expert", None, ("dp", "tensor")),
            P("expert", None, ("dp", "tensor")),
            P("expert", ("dp", "tensor"), None),
        ),
        out_specs=(P(("expert", "tensor"), None), P(("expert", "tensor"), None)),
        check_vma=False,
    )
```
